32 devices in a mesh: fsdp: 4 (over y, x), ctx: 8 (over z, core).
Axes of the slice: x: 2, y: 2, z: 4, core: 2. Of those that a mesh axis runs over, the one named last changes fastest.
Arguments:
- tokens: bfloat16 [4096, 1024], P(('fsdp', 'ctx')), may hold values from -24 to 24
- pairs: int32 [8, 2], replicated, may hold values from 0 to 15, as said below
- ln1_gain: bfloat16 [1, 1024], P(None, 'fsdp'), may hold values from 0.5 to 1.5
- ln1_bias: bfloat16 [1, 1024], P(None, 'fsdp'), may hold values from -1.75 to 1.75
- qkv_weight: bfloat16 [1, 1024, 3072], P(None, 'fsdp'), may hold values from -2 to 2
- qv_bias: bfloat16 [1, 2, 1024], P(None, None, 'fsdp'), may hold values from -3 to 3
- out_weight: bfloat16 [1, 1024, 1024], P(None, 'fsdp'), may hold values from -1.5 to 1.5
- out_bias: bfloat16 [1, 1024], P(None, 'fsdp'), may hold values from -1.75 to 1.75
- ln2_gain: bfloat16 [1, 1024], P(None, 'fsdp'), may hold values from 0.5 to 1.5
- ln2_bias: bfloat16 [1, 1024], P(None, 'fsdp'), may hold values from -1.75 to 1.75
- fc_weight: bfloat16 [1, 1024, 4096], P(None, 'fsdp'), may hold values from -0.1875 to 0.1875
- fc_bias: bfloat16 [1, 4096], P(None, 'fsdp'), may hold values from -3 to 3
- proj_weight: bfloat16 [1, 4096, 1024], P(None, None, 'fsdp'), may hold values from -0.09375 to 0.09375
- proj_bias: bfloat16 [1, 1024], P(None, 'fsdp'), may hold values from -1.75 to 1.75
- cotangent: float32 [4096, 1024], P(('fsdp', 'ctx')), may hold values from -12 to 12
Outputs:
- output: bfloat16 [4096, 1024], P(('fsdp', 'ctx'))
- tokens_grad: float32 [4096, 1024], P(('fsdp', 'ctx'))
- ln1_gain_grad: float32 [1, 1024], P(None, 'fsdp')
- ln1_bias_grad: float32 [1, 1024], P(None, 'fsdp')
- qkv_weight_grad: float32 [1, 1024, 3072], P(None, 'fsdp')
- qv_bias_grad: float32 [1, 2, 1024], P(None, None, 'fsdp')
- out_weight_grad: float32 [1, 1024, 1024], P(None, 'fsdp')
- out_bias_grad: float32 [1, 1024], P(None, 'fsdp')
- ln2_gain_grad: float32 [1, 1024], P(None, 'fsdp')
- ln2_bias_grad: float32 [1, 1024], P(None, 'fsdp')
- fc_weight_grad: float32 [1, 1024, 4096], P(None, 'fsdp')
- fc_bias_grad: float32 [1, 4096], P(None, 'fsdp')
- proj_weight_grad: float32 [1, 4096, 1024], P(None, None, 'fsdp')
- proj_bias_grad: float32 [1, 1024], P(None, 'fsdp')
The draws below stay inside these ranges and needn't reach their ends.
Inputs may be any that keep to these rules, and one draw needn't show every extreme that they name: `pairs`: row c holds a block b and its mirror 16 - 1 - b, in either order; every block appears once.
All inputs are finite; a program needn't handle non-finite values.
Results may differ from the reference program's by a relative error of at most 0.0096.
Values may be sent and summed in bfloat16 or wider, within the bound.
No kernel may reach another device: no remote copies, remote signals or barrier semaphores. Data moves between devices by JAX's collectives and lax.ppermute only.
A program may use at most 192 MiB of HBM per device.

```python
import math
import jax
import jax.numpy as jnp
from jax import lax

D = 1024
HEADS = 16
HEAD_DIM = 64
FF = 4096
LAYERS = 1
TOK_DEV = 128
BLK = 64
BLOCKS = 16
LENGTH = 1024
SEQS = 4
TOKENS = 4096
N_CTX = 8


def draw_tokens(key, part):
    key_base, key_cols, key_rows = jax.random.split(key, 3)
    col_scale = jnp.exp(jax.random.uniform(key_cols, (1, D), jnp.float32, math.log(0.3), math.log(3.0)))
    row_scale = jnp.exp(jax.random.uniform(key_rows, (TOKENS, 1), jnp.float32, math.log(0.3), math.log(3.0)))
    base = jax.random.normal(key_base, (TOKENS, D), jnp.float32)
    return jnp.clip(base * col_scale * row_scale, -24.0, 24.0).astype(jnp.bfloat16)


def draw_pairs(key, part):
    order = jax.random.permutation(jax.random.fold_in(key, 11), N_CTX).astype(jnp.int32)
    flip = jax.random.randint(jax.random.fold_in(key, 12), (N_CTX,), 0, 2, jnp.int32)
    mirror = (BLOCKS - 1 - order).astype(jnp.int32)
    first = jnp.where(flip == 1, mirror, order)
    second = jnp.where(flip == 1, order, mirror)
    return jnp.stack([first, second], axis=1).astype(jnp.int32)


def draw_qkv_weight(key, part):
    key_base = jax.random.fold_in(key, 0)
    base = jax.random.normal(key_base, (LAYERS, D, 3 * D), jnp.float32) * D ** (-0.5)
    return jnp.clip(base, -2.0, 2.0).astype(jnp.bfloat16)


def with_spikes(values, stream_key, source, target, blocks, factor):
    owner, partner = [(jnp.arange(values.shape[axis_at]) // (values.shape[axis_at] // blocks)).reshape([-1 if axis == axis_at else 1 for axis in range(values.ndim)]) for axis_at in (source, target)]
    chosen = jax.random.permutation(stream_key, blocks)[partner]
    strong = (owner == chosen) | (owner == (partner + blocks // 2) % blocks)
    return jnp.where(strong, factor * values, values)


def block_scale(rng, dims, cuts, low, largest):
    loudness, own = 1.0, jax.random.fold_in(rng, 6)
    for axis_at, shards_of in cuts:
        heights = jnp.exp(jax.random.uniform(jax.random.fold_in(own, axis_at), (shards_of,), jnp.float32, low / len(cuts), largest / len(cuts)))
        loudness = loudness * jnp.repeat(heights, dims[axis_at] // shards_of).reshape([-1 if axis == axis_at else 1 for axis in range(len(dims))])
    return loudness


def centred(key, dims, scale, most, shards=(), held_as=jnp.bfloat16):
    level = block_scale(key, dims, shards, -0.22, 0.18) if shards else 1.0
    drawn = jax.random.normal(key, dims, jnp.float32) * scale * level
    return jnp.minimum(jnp.maximum(drawn, -most), most).astype(held_as)


def bell_draw_with(stream_key, shape, scale, limit, pieces, heavy, kind=jnp.bfloat16):
    result = scale * jax.random.normal(stream_key, shape, jnp.float32)
    if pieces:
        result = result * block_scale(stream_key, shape, pieces, -0.22, 0.18)
    return jnp.clip(with_spikes(result, jax.random.fold_in(stream_key, 3), *heavy), -limit, limit).astype(kind)


def setup_inputs(seed: int = 0) -> dict:
    arg_keys = jax.random.split(jax.random.key(seed), 16)
    return {
        "tokens": draw_tokens(jax.random.fold_in(arg_keys[15], 71), 0),
        "pairs": draw_pairs(jax.random.fold_in(arg_keys[15], 71), 0),
        "ln1_gain": jnp.clip(1.0 + 0.1 * jax.random.normal(arg_keys[2], (LAYERS, D), jnp.float32), 0.5, 1.5).astype(jnp.bfloat16),
        "ln1_bias": centred(arg_keys[3], (LAYERS, D), 0.3, 1.75, ((1, 4),)),
        "qkv_weight": draw_qkv_weight(jax.random.fold_in(arg_keys[15], 71), 0),
        "qv_bias": centred(arg_keys[5], (LAYERS, 2, D), 0.5, 3.0, ((2, 4),)),
        "out_weight": centred(arg_keys[6], (LAYERS, D, D), (D // 64) ** -0.5, 1.5, ((1, 4),)),
        "out_bias": centred(arg_keys[7], (LAYERS, D), 0.3, 1.75, ((1, 4),)),
        "ln2_gain": jnp.clip(1.0 + 0.1 * jax.random.normal(arg_keys[8], (LAYERS, D), jnp.float32), 0.5, 1.5).astype(jnp.bfloat16),
        "ln2_bias": centred(arg_keys[9], (LAYERS, D), 0.3, 1.75, ((1, 4),)),
        "fc_weight": centred(arg_keys[10], (LAYERS, D, FF), D ** -0.5, 0.1875, ((1, 4),)),
        "fc_bias": centred(arg_keys[11], (LAYERS, FF), 0.5, 3.0, ((1, 4),)),
        "proj_weight": centred(arg_keys[12], (LAYERS, FF, D), FF ** -0.5, 0.09375, ((2, 4),)),
        "proj_bias": centred(arg_keys[13], (LAYERS, D), 0.3, 1.75, ((1, 4),)),
        "cotangent": bell_draw_with(arg_keys[14], (TOKENS, D), 1.0, 12.0, ((0, 32),), (0, 1, 32, 2.75), jnp.float32),
    }


LN_EPS = 1e-05
GELU_SCALE = 0.7978845608028654
GELU_CUBIC = 0.044715
MASKED = -1e+30

def contract_rows(left, right):
    return lax.dot_general(left, right, (((0,), (0,)), ((), ())), preferred_element_type=jnp.float32)

def times_transpose(left, right):
    return lax.dot_general(left, right, (((1,), (1,)), ((), ())), preferred_element_type=jnp.float32)

def layer_norm(stream, gain, shift):
    centre = stream - lax.optimization_barrier(jnp.mean(stream, axis=1, keepdims=True))
    inv_std = lax.rsqrt(lax.optimization_barrier(jnp.mean(centre * centre, axis=1, keepdims=True)) + LN_EPS)
    normed = centre * inv_std
    return (normed, inv_std, (normed * gain.astype(jnp.float32) + shift.astype(jnp.float32)).astype(jnp.bfloat16))

def norm_backward(act_grad, normed, inv_std, gain):
    scaled = act_grad * gain.astype(jnp.float32)
    stream_grad = inv_std * (scaled - lax.optimization_barrier(jnp.mean(scaled, axis=1, keepdims=True)) - normed * lax.optimization_barrier(jnp.mean(scaled * normed, axis=1, keepdims=True)))
    return (stream_grad, lax.optimization_barrier(jnp.sum(act_grad * normed, axis=0)), lax.optimization_barrier(jnp.sum(act_grad, axis=0)))

def gelu_parts(pre):
    inner = GELU_SCALE * (pre + GELU_CUBIC * pre * pre * pre)
    tangent = jnp.tanh(inner)
    value = 0.5 * pre * (1.0 + tangent)
    slope = 0.5 * (1.0 + tangent) + 0.5 * pre * (1.0 - tangent * tangent) * GELU_SCALE * (1.0 + 3.0 * GELU_CUBIC * pre * pre)
    return (value, slope)

def head_split(rows):
    return rows.reshape(rows.shape[0], HEADS, HEAD_DIM).transpose(1, 0, 2)

def head_join(stacked):
    return stacked.transpose(1, 0, 2).reshape(stacked.shape[1], HEADS * HEAD_DIM)

def attend(query, keys, values, allowed):
    scale = HEAD_DIM ** (-0.5)

    def one_head(parts):
        q_head, k_head, v_head = parts
        scores = jnp.where(allowed, times_transpose(q_head, k_head) * scale, MASKED)
        peak = lax.optimization_barrier(jnp.max(scores, axis=1, keepdims=True))
        expo = jnp.exp(scores - peak)
        total = lax.optimization_barrier(jnp.sum(expo, axis=1, keepdims=True))
        weights = (expo / total).astype(jnp.bfloat16)
        mixed = jnp.dot(weights, v_head, preferred_element_type=jnp.float32)
        return (mixed.astype(jnp.bfloat16), (peak + jnp.log(total))[:, 0])
    outs, log_total = lax.map(one_head, (head_split(query), head_split(keys), head_split(values)))
    return (head_join(outs), log_total)

def attend_back(query, keys, values, attended, attended_grad, log_total, allowed):
    scale = HEAD_DIM ** (-0.5)

    def one_head(parts):
        q_head, k_head, v_head, o_head, do_head, lse_head = parts
        scores = jnp.where(allowed, times_transpose(q_head, k_head) * scale, MASKED)
        prob = jnp.exp(scores - lse_head[:, None])
        values_grad = contract_rows(prob.astype(jnp.bfloat16), do_head)
        prob_grad = times_transpose(do_head, v_head)
        delta = lax.optimization_barrier(jnp.sum(do_head.astype(jnp.float32) * o_head.astype(jnp.float32), axis=1, keepdims=True))
        score_low = (prob * (prob_grad - delta)).astype(jnp.bfloat16)
        query_grad = jnp.dot(score_low, k_head, preferred_element_type=jnp.float32) * scale
        keys_grad = contract_rows(score_low, q_head) * scale
        return (query_grad, keys_grad, values_grad)
    grads = lax.map(one_head, (head_split(query), head_split(keys), head_split(values), head_split(attended), head_split(attended_grad), log_total))
    return (head_join(grads[0]), head_join(grads[1]), head_join(grads[2]))

def run_sequence(rows, upstream, params, allowed):
    ln1_gain, ln1_bias, qkv_weight, qv_bias, out_weight, out_bias, ln2_gain, ln2_bias, fc_weight, fc_bias, proj_weight, proj_bias = params
    width = rows.shape[1]
    stream = rows.astype(jnp.float32)
    saved = []
    for layer in range(LAYERS):
        normed_one, inv_one, act_one = layer_norm(stream, ln1_gain[layer], ln1_bias[layer])
        mixed = jnp.dot(act_one, qkv_weight[layer], preferred_element_type=jnp.float32)
        query = (mixed[:, :width] + qv_bias[layer, 0].astype(jnp.float32)).astype(jnp.bfloat16)
        keys = mixed[:, width:2 * width].astype(jnp.bfloat16)
        values = (mixed[:, 2 * width:] + qv_bias[layer, 1].astype(jnp.float32)).astype(jnp.bfloat16)
        attended, log_total = attend(query, keys, values, allowed)
        stream_mid = stream + jnp.dot(attended, out_weight[layer], preferred_element_type=jnp.float32) + out_bias[layer].astype(jnp.float32)
        normed_two, inv_two, act_two = layer_norm(stream_mid, ln2_gain[layer], ln2_bias[layer])
        pre = jnp.dot(act_two, fc_weight[layer], preferred_element_type=jnp.float32) + fc_bias[layer].astype(jnp.float32)
        value, slope = gelu_parts(pre)
        hidden = value.astype(jnp.bfloat16)
        stream = stream_mid + jnp.dot(hidden, proj_weight[layer], preferred_element_type=jnp.float32) + proj_bias[layer].astype(jnp.float32)
        saved.append((normed_one, inv_one, act_one, query, keys, values, attended, log_total, normed_two, inv_two, act_two, slope, hidden))
    grad = upstream
    layer_grads = []
    for layer in reversed(range(LAYERS)):
        normed_one, inv_one, act_one, query, keys, values, attended, log_total, normed_two, inv_two, act_two, slope, hidden = saved[layer]
        grad_low = grad.astype(jnp.bfloat16)
        proj_grad = contract_rows(hidden, grad_low)
        proj_bias_grad = lax.optimization_barrier(jnp.sum(grad, axis=0))
        pre_grad = times_transpose(grad_low, proj_weight[layer]) * slope
        pre_low = pre_grad.astype(jnp.bfloat16)
        fc_grad = contract_rows(act_two, pre_low)
        fc_bias_grad = lax.optimization_barrier(jnp.sum(pre_grad, axis=0))
        act_two_grad = times_transpose(pre_low, fc_weight[layer])
        stream_part, gain_two_grad, shift_two_grad = norm_backward(act_two_grad, normed_two, inv_two, ln2_gain[layer])
        grad_mid = grad + stream_part
        mid_low = grad_mid.astype(jnp.bfloat16)
        out_grad = contract_rows(attended, mid_low)
        out_bias_grad = lax.optimization_barrier(jnp.sum(grad_mid, axis=0))
        attended_grad = times_transpose(mid_low, out_weight[layer]).astype(jnp.bfloat16)
        query_grad, keys_grad, values_grad = attend_back(query, keys, values, attended, attended_grad, log_total, allowed)
        mixed_low = jnp.concatenate([query_grad, keys_grad, values_grad], axis=1).astype(jnp.bfloat16)
        qkv_grad = contract_rows(act_one, mixed_low)
        qv_grad = jnp.stack([lax.optimization_barrier(jnp.sum(query_grad, axis=0)), lax.optimization_barrier(jnp.sum(values_grad, axis=0))])
        act_one_grad = times_transpose(mixed_low, qkv_weight[layer])
        stream_part, gain_one_grad, shift_one_grad = norm_backward(act_one_grad, normed_one, inv_one, ln1_gain[layer])
        grad = grad_mid + stream_part
        layer_grads.insert(0, (gain_one_grad, shift_one_grad, qkv_grad, qv_grad, out_grad, out_bias_grad, gain_two_grad, shift_two_grad, fc_grad, fc_bias_grad, proj_grad, proj_bias_grad))
    stacked = tuple((jnp.stack([layer_grads[layer][index] for layer in range(LAYERS)]) for index in range(12)))
    return (stream.astype(jnp.bfloat16), grad, stacked)

def sequence_positions(pairs):
    rows = jnp.arange(TOK_DEV * N_CTX, dtype=jnp.int32)
    local = rows % TOK_DEV
    block = pairs[rows // TOK_DEV, local // BLK]
    return (block * BLK + local % BLK).astype(jnp.int32)

def reference(tokens, pairs, ln1_gain, ln1_bias, qkv_weight, qv_bias, out_weight, out_bias, ln2_gain, ln2_bias, fc_weight, fc_bias, proj_weight, proj_bias, cotangent):
    params = (ln1_gain, ln1_bias, qkv_weight, qv_bias, out_weight, out_bias, ln2_gain, ln2_bias, fc_weight, fc_bias, proj_weight, proj_bias)
    positions = sequence_positions(pairs)
    allowed = positions[None, :] <= positions[:, None]
    seq_tokens = tokens.reshape(SEQS, LENGTH, D)
    seq_upstream = cotangent.reshape(SEQS, LENGTH, D)
    zero_grads = tuple((jnp.zeros(param.shape, jnp.float32) for param in params))

    def one_sequence(totals, inputs):
        rows, upstream = inputs
        out_rows, in_grad, grads = run_sequence(rows, upstream, params, allowed)
        return (tuple((left + right for left, right in zip(totals, grads))), (out_rows, in_grad))
    totals, (outputs, input_grads) = lax.scan(one_sequence, zero_grads, (seq_tokens, seq_upstream))
    return (outputs.reshape(TOKENS, D), input_grads.reshape(TOKENS, D), totals[0], totals[1], totals[2], totals[3], totals[4], totals[5], totals[6], totals[7], totals[8], totals[9], totals[10], totals[11])
```

```python
import functools

import jax
import jax.numpy as jnp
from jax import lax
from jax.experimental import pallas as pl
from jax.experimental.pallas import tpu as pltpu
from jax.sharding import Mesh, PartitionSpec as P

HEADS = 16
HEAD_DIM = 64

LN_EPS = 1e-05
GELU_SCALE = 0.7978845608028654
GELU_CUBIC = 0.044715
MASKED = -1e30

F32 = jnp.float32
BF16 = jnp.bfloat16


ZAX = ("h", "l")
CTX = ("h", "l", "c")


GROUP = ("c", "l", "h")
NEAR = ("c", "l")


def swap(x, axis, bit):
    n = lax.axis_size(axis)
    return lax.ppermute(x, axis, [(i, i ^ bit) for i in range(n)])


def bits(axes):
    out = []
    for axis in reversed(axes):
        bit = 1
        while bit < lax.axis_size(axis):
            out.append((axis, bit))
            bit *= 2
    return out


def gather(x, axes):
    x = x[None]
    for axis, bit in bits(axes):
        x = jnp.concatenate([x, swap(x, axis, bit)], axis=0)
    return x


def scatter_sum(x, axes):
    for axis, bit in reversed(bits(axes)):
        size = x.shape[0] // 2
        x = x[:size].astype(F32) + swap(x[size:].astype(BF16), axis, bit).astype(F32)
    return x[0]


def exchange(x, axes):
    tail = x.shape[1:]
    after = 1
    for axis, bit in bits(axes):
        y = x.reshape(x.shape[0] // (2 * after), 2, after, *tail)
        away = swap(y[:, 1], axis, bit)
        x = jnp.stack([y[:, 0], away], axis=1).reshape(x.shape)
        after *= 2
    return x


def fsdp_swap(x, step):
    nf = lax.axis_size("f")
    steps = nf.bit_length() - 1
    bit = lambda c: 1 << (step if c == 0 else steps - 1 - step)
    return lax.ppermute(x, ("f", "c"), [(2 * i + c, 2 * (i ^ bit(c)) + c) for i in range(nf) for c in range(2)])


def fsdp_order(x):
    nf = x.shape[0]
    steps = nf.bit_length() - 1
    first = lax.axis_index("c") == 0
    turn = lambda t: sum(((t >> i) & 1) << (steps - 1 - i) for i in range(steps))
    return jnp.stack([x[t] if turn(t) == t else jnp.where(first, x[t], x[turn(t)]) for t in range(nf)])


def fsdp_gather(x):
    x = x[None]
    for step in range(lax.axis_size("f").bit_length() - 1):
        x = jnp.concatenate([x, fsdp_swap(x, step)], axis=0)
    return fsdp_order(x)


def fsdp_sum_step(x, step):
    size = x.shape[0] // 2
    return x[:size].astype(F32) + fsdp_swap(x[size:].astype(BF16), step).astype(F32)


def fsdp_sum(x):
    for step in reversed(range(lax.axis_size("f").bit_length() - 1)):
        x = fsdp_sum_step(x, step)
    return x[0]


def after(x, *others):
    return lax.optimization_barrier((x, *others))[0]


def relative(x, index, n):
    size = x.shape[1] // n
    blocks = [x[:, i * size : (i + 1) * size] for i in range(n)]
    bit = 1
    while bit < n:
        turned = (index & bit) != 0
        blocks = [jnp.where(turned, blocks[i ^ bit], blocks[i]) for i in range(n)]
        bit *= 2
    return jnp.concatenate(blocks, axis=1)


def dot(left, right, dims):
    return lax.dot_general(left, right, (dims, ((), ())), preferred_element_type=F32)


def matmul(left, right):
    return dot(left, right, ((1,), (0,)))


def times_transpose(left, right):
    return dot(left, right, ((1,), (1,)))


def contract_rows(left, right):
    return dot(left, right, ((0,), (0,)))


def layer_norm(stream, gain, shift):
    centre = stream - jnp.mean(stream, axis=1, keepdims=True)
    inv_std = lax.rsqrt(jnp.mean(centre * centre, axis=1, keepdims=True) + LN_EPS)
    normed = centre * inv_std
    return normed, inv_std, (normed * gain + shift).astype(BF16)


def norm_backward(act_grad, normed, inv_std, gain):
    scaled = act_grad * gain
    stream_grad = inv_std * (
        scaled
        - jnp.mean(scaled, axis=1, keepdims=True)
        - normed * jnp.mean(scaled * normed, axis=1, keepdims=True)
    )
    return (
        stream_grad,
        jnp.sum(act_grad * normed, axis=0, keepdims=True),
        jnp.sum(act_grad, axis=0, keepdims=True),
    )


def gelu_parts(pre):
    inner = GELU_SCALE * (pre + GELU_CUBIC * pre * pre * pre)
    tangent = jnp.tanh(inner)
    value = 0.5 * pre * (1.0 + tangent)
    slope = 0.5 * (1.0 + tangent) + 0.5 * pre * (1.0 - tangent * tangent) * GELU_SCALE * (
        1.0 + 3.0 * GELU_CUBIC * pre * pre
    )
    return value, slope


def key_positions(count, rows_dev, me_ref, pairs_ref):
    half = rows_dev // 2
    at = lax.broadcasted_iota(jnp.int32, (1, count), 1)
    block = jnp.zeros((1, count), jnp.int32)
    for s in range(count // half):
        block = jnp.where(at // half == s, pairs_ref[(s // 2) ^ me_ref[0], s % 2], block)
    return block * half + at % half


def query_positions(first, rows, rows_dev, me_ref, pairs_ref):
    half = rows_dev // 2
    at = lax.broadcasted_iota(jnp.int32, (rows, 1), 0)
    block = jnp.zeros((rows, 1), jnp.int32)
    for s in range(rows // half):
        member = (first // rows_dev + s // 2) ^ me_ref[0]
        block = jnp.where(at // half == s, pairs_ref[member, s % 2], block)
    return block * half + at % half


def attend_kernel(rows, heads, rows_dev, me_ref, pairs_ref, qkv_ref, out_ref, lse_ref):
    width = heads * HEAD_DIM
    scale = HEAD_DIM ** (-0.5)
    keys = qkv_ref[:, width : 2 * width]
    values = qkv_ref[:, 2 * width : 3 * width]
    kpos = key_positions(qkv_ref.shape[0], rows_dev, me_ref, pairs_ref)
    owner = lax.broadcasted_iota(jnp.int32, (rows, width), 1) // HEAD_DIM

    def step(i, carry):
        at = pl.ds(pl.multiple_of(i * rows, rows), rows)
        query = qkv_ref[at, 0:width]
        allowed = kpos <= query_positions(i * rows, rows, rows_dev, me_ref, pairs_ref)
        out = jnp.zeros((rows, width), F32)
        lse = jnp.zeros((rows, width), F32)
        for h in range(heads):
            mine = owner == h
            q_head = jnp.where(mine, query, jnp.zeros_like(query))
            scores = times_transpose(q_head, keys) * scale
            scores = jnp.where(allowed, scores, MASKED)
            peak = jnp.max(scores, axis=1, keepdims=True)
            expo = jnp.exp(scores - peak)
            total = jnp.sum(expo, axis=1, keepdims=True)
            weights = (expo * (1.0 / total)).astype(BF16)
            out = jnp.where(mine, matmul(weights, values), out)
            lse = jnp.where(mine, peak + jnp.log(total), lse)
        out_ref[at, :] = out.astype(BF16)
        lse_ref[at, :] = lse
        return carry

    lax.fori_loop(0, qkv_ref.shape[0] // rows, step, 0)


def attend_back_kernel(
    rows, heads, rows_dev, me_ref, pairs_ref, qkv_ref, att_ref, grad_ref, lse_ref,
    low_ref, sums_ref, dk_ref, dv_ref, qsum_ref,
):
    width = heads * HEAD_DIM
    scale = HEAD_DIM ** (-0.5)
    keys = qkv_ref[:, width : 2 * width]
    values = qkv_ref[:, 2 * width : 3 * width]
    kpos = key_positions(qkv_ref.shape[0], rows_dev, me_ref, pairs_ref)
    owner = lax.broadcasted_iota(jnp.int32, (rows, width), 1) // HEAD_DIM
    dk_ref[...] = jnp.zeros_like(dk_ref)
    dv_ref[...] = jnp.zeros_like(dv_ref)
    qsum_ref[...] = jnp.zeros_like(qsum_ref)

    def step(i, carry):
        at = pl.ds(pl.multiple_of(i * rows, rows), rows)
        query = qkv_ref[at, 0:width]
        upstream = grad_ref[at, :]
        product = upstream.astype(F32) * att_ref[at, :].astype(F32)
        lse = lse_ref[at, :]
        allowed = kpos <= query_positions(i * rows, rows, rows_dev, me_ref, pairs_ref)
        dq = jnp.zeros((rows, width), F32)
        for h in range(heads):
            mine = owner == h
            q_head = jnp.where(mine, query, jnp.zeros_like(query))
            do_head = jnp.where(mine, upstream, jnp.zeros_like(upstream))
            delta = jnp.sum(jnp.where(mine, product, 0.0), axis=1, keepdims=True)
            lse_head = jnp.max(jnp.where(mine, lse, -3e38), axis=1, keepdims=True)
            scores = times_transpose(q_head, keys) * scale
            scores = jnp.where(allowed, scores, MASKED)
            prob = jnp.exp(scores - lse_head)
            dv_ref[...] += contract_rows(prob.astype(BF16), do_head)
            prob_grad = times_transpose(do_head, values)
            score_low = (prob * (prob_grad - delta)).astype(BF16)
            dk_ref[...] += contract_rows(score_low, q_head) * scale
            dq = jnp.where(mine, matmul(score_low, keys) * scale, dq)
        low_ref[at, 0:width] = dq.astype(BF16)
        qsum_ref[...] += jnp.sum(dq, axis=0, keepdims=True)
        return carry

    lax.fori_loop(0, qkv_ref.shape[0] // rows, step, 0)
    low_ref[:, width : 2 * width] = dk_ref[...].astype(BF16)
    low_ref[:, 2 * width : 3 * width] = dv_ref[...].astype(BF16)
    sums_ref[0:1, :] = qsum_ref[...]
    sums_ref[1:2, :] = jnp.sum(dv_ref[...], axis=0, keepdims=True)


def in_smem_then_vmem(n):
    return [pl.BlockSpec(memory_space=pltpu.SMEM)] * 2 + [pl.BlockSpec(memory_space=pltpu.VMEM)] * n


def attend(me, pairs, qkv, heads, rows_dev):
    count, width = qkv.shape[0], heads * HEAD_DIM
    return pl.pallas_call(
        functools.partial(attend_kernel, 256, heads, rows_dev),
        in_specs=in_smem_then_vmem(1),
        out_shape=(
            jax.ShapeDtypeStruct((count, width), BF16),
            jax.ShapeDtypeStruct((count, width), F32),
        ),
        cost_estimate=pl.CostEstimate(
            flops=4 * count * count * width, bytes_accessed=count * width * 12, transcendentals=count * count * heads
        ),
        name="attend",
    )(me, pairs, qkv)


def attend_back(me, pairs, qkv, att, grad, lse, heads, rows_dev):
    count, width = qkv.shape[0], heads * HEAD_DIM
    return pl.pallas_call(
        functools.partial(attend_back_kernel, 256, heads, rows_dev),
        in_specs=in_smem_then_vmem(4),
        out_shape=(
            jax.ShapeDtypeStruct((count, 3 * width), BF16),
            jax.ShapeDtypeStruct((2, width), F32),
        ),
        scratch_shapes=[
            pltpu.VMEM((count, width), F32),
            pltpu.VMEM((count, width), F32),
            pltpu.VMEM((1, width), F32),
        ],
        cost_estimate=pl.CostEstimate(
            flops=10 * count * count * width, bytes_accessed=count * width * 20, transcendentals=count * count * heads
        ),
        name="attend_back",
    )(me, pairs, qkv, att, grad, lse)


def place_mlp_kernel(me_ref, all_ref, fc_ref, proj_ref):
    fc_ref[...] = all_ref[0].astype(F32)
    proj_ref[...] = all_ref[1].astype(F32).T


def place_mlp(me, gathered):
    nc, _, shard, piece = gathered.shape
    size = gathered.size
    return pl.pallas_call(
        place_mlp_kernel,
        grid_spec=pltpu.PrefetchScalarGridSpec(
            num_scalar_prefetch=1,
            grid=(nc,),
            in_specs=[pl.BlockSpec((None, 2, shard, piece), lambda i, me: (i ^ me[0], 0, 0, 0))],
            out_specs=[
                pl.BlockSpec((shard, piece), lambda i, me: (0, i)),
                pl.BlockSpec((piece, shard), lambda i, me: (i, 0)),
            ],
        ),
        out_shape=[
            jax.ShapeDtypeStruct((shard, nc * piece), F32),
            jax.ShapeDtypeStruct((nc * piece, shard), F32),
        ],
        cost_estimate=pl.CostEstimate(flops=size, bytes_accessed=size * 6, transcendentals=0),
        name="place_mlp",
    )(me, gathered)


def place_attention_kernel(hw, me_ref, all_ref, qkv_ref, out_ref):
    nc = all_ref.shape[0]
    for i in range(nc):
        r = i ^ me_ref[0]
        for part in range(3):
            at = (part * nc + i) * hw
            qkv_ref[:, at : at + hw] = all_ref[r, :, part * hw : (part + 1) * hw].astype(F32)
        out_ref[:, i * hw : (i + 1) * hw] = all_ref[r, :, 3 * hw : 4 * hw].astype(F32)


def place_attention(me, gathered, hw):
    nc, shard, _ = gathered.shape
    size = gathered.size
    return pl.pallas_call(
        functools.partial(place_attention_kernel, hw),
        in_specs=[pl.BlockSpec(memory_space=pltpu.SMEM), pl.BlockSpec(memory_space=pltpu.VMEM)],
        out_shape=[
            jax.ShapeDtypeStruct((shard, 3 * nc * hw), F32),
            jax.ShapeDtypeStruct((shard, nc * hw), F32),
        ],
        cost_estimate=pl.CostEstimate(flops=size, bytes_accessed=size * 6, transcendentals=0),
        name="place_attention",
    )(me, gathered)


def body(
    tokens,
    pairs,
    ln1_gain,
    ln1_bias,
    qkv_weight,
    qv_bias,
    out_weight,
    out_bias,
    ln2_gain,
    ln2_bias,
    fc_weight,
    fc_bias,
    proj_weight,
    proj_bias,
    cotangent,
):
    nf, nh, nl = lax.axis_size("f"), lax.axis_size("h"), lax.axis_size("l")
    nm, nc = 2 * nl, 2 * nl * nh
    f, h, l, c = (lax.axis_index(a) for a in ("f", "h", "l", "c"))
    m = c * nl + l
    j = m * nh + h
    rows, width = tokens.shape
    shard = width // nf
    heads = HEADS // nc
    hw = heads * HEAD_DIM
    ff = fc_weight.shape[2] // nm
    piece = ff // nh
    fb = fc_bias.shape[1] // shard
    me = jnp.reshape(j, (1,)).astype(jnp.int32)
    pairs = pairs.reshape(nh, nl, 2, 2).transpose(2, 1, 0, 3).reshape(nc, 2)

    vectors = jnp.concatenate(
        [ln1_gain, ln1_bias, ln2_gain, ln2_bias, out_bias, proj_bias, qv_bias[0], fc_bias.reshape(fb, shard)],
        axis=0,
    )
    vec_parts = fsdp_gather(vectors)
    vec = jnp.concatenate([vec_parts[r] for r in range(nf)], axis=1).astype(F32)
    gain_one, shift_one, gain_two, shift_two, bias_out, bias_proj = (vec[i : i + 1] for i in range(6))

    wq_own = jnp.concatenate(
        [lax.dynamic_slice(qkv_weight[0], (0, i * width + j * hw), (shard, hw)) for i in range(3)], axis=1
    )
    w_qkv = fsdp_gather(wq_own).reshape(width, 3 * hw)
    w_out = fsdp_gather(after(out_weight[0], w_qkv)).reshape(width, width)
    mlp_own = jnp.stack(
        [
            lax.dynamic_slice(fc_weight[0], (0, m * ff), (shard, ff)),
            lax.dynamic_slice(proj_weight[0], (m * ff, 0), (ff, shard)).T,
        ]
    )
    mlp_all = fsdp_gather(after(mlp_own, w_out))
    w_fc, w_proj = mlp_all[:, 0].reshape(width, ff), mlp_all[:, 1].reshape(width, ff)

    bias_qv = relative(vec[6:8], f, nf)
    bias_q = lax.dynamic_slice(bias_qv, (0, j * hw), (1, hw))
    bias_v = lax.dynamic_slice(bias_qv, (1, j * hw), (1, hw))
    bias_mixed = jnp.concatenate([bias_q, jnp.zeros((1, hw), F32), bias_v], axis=1)
    fc_rel = jnp.concatenate([vec_parts[r, 8:].reshape(1, fb * shard) for r in range(nf)], axis=1)
    bias_fc = lax.dynamic_slice(relative(fc_rel, f, nf), (0, m * ff), (1, ff)).astype(F32)

    stream = relative(tokens, f, nf).astype(F32)
    grad = relative(cotangent, f, nf)

    normed_one, inv_one, act_one = layer_norm(stream, gain_one, shift_one)
    act_one_all = gather(act_one, GROUP).reshape(nc * rows, width)
    qkv = (matmul(act_one_all, w_qkv) + bias_mixed).astype(BF16)
    att, lse = attend(me, pairs, qkv, heads, rows)

    def rows_from_heads(x):
        x = exchange(x.reshape(nc, rows, hw), GROUP)
        return relative(jnp.concatenate([x[r] for r in range(nc)], axis=1), j, nc)

    def heads_from_rows(x):
        x = relative(x, j, nc)
        x = jnp.stack([x[:, r * hw : (r + 1) * hw] for r in range(nc)])
        return exchange(x, GROUP).reshape(nc * rows, hw)

    attended = relative(rows_from_heads(att), f, nf)
    stream_mid = stream + relative(matmul(attended, w_out), f, nf) + bias_out
    normed_two, inv_two, act_two = layer_norm(stream_mid, gain_two, shift_two)
    act_two_all = gather(act_two, NEAR).reshape(nm * rows, width)
    pre = matmul(act_two_all, w_fc) + bias_fc
    value, slope = gelu_parts(pre)
    hidden = value.astype(BF16)

    grad_low = after(grad.astype(BF16), act_one_all)
    grad_all = gather(grad_low, NEAR).reshape(nm * rows, width)
    pre_grad = matmul(grad_all, w_proj) * slope
    pre_low = pre_grad.astype(BF16)
    fc_bias_grad = jnp.sum(pre_grad, axis=0, keepdims=True)
    act_two_grad = scatter_sum(times_transpose(pre_low, w_fc).reshape(nm, rows, width), NEAR)

    mlp_chunks = jnp.stack(
        [
            contract_rows(act_two_all, pre_low).astype(BF16).reshape(nf, shard, ff),
            contract_rows(grad_all, hidden).astype(BF16).reshape(nf, shard, ff),
        ],
        axis=1,
    )
    mlp_chunks = fsdp_order(mlp_chunks)
    act_two_grad = after(act_two_grad, mlp_chunks)
    last = nf.bit_length() - 2
    mlp_sum = fsdp_sum_step(mlp_chunks, last)

    stream_part, gain_two_grad, shift_two_grad = norm_backward(act_two_grad, normed_two, inv_two, gain_two)
    grad_mid = grad + stream_part
    mid_low = grad_mid.astype(BF16)
    mid_natural = relative(mid_low, f, nf)
    att_grad = heads_from_rows(relative(times_transpose(mid_natural, w_out).astype(BF16), f, nf))

    att_grad = after(att_grad, mlp_sum)
    for step in reversed(range(last)):
        mlp_sum = fsdp_sum_step(mlp_sum, step)
    mlp_sum = mlp_sum[0]

    mixed_low, qv_sums = attend_back(me, pairs, qkv, att, att_grad, lse, heads, rows)
    act_one_grad = scatter_sum(times_transpose(mixed_low, w_qkv).reshape(nc, rows, width), GROUP)
    stream_part, gain_one_grad, shift_one_grad = norm_backward(act_one_grad, normed_one, inv_one, gain_one)
    tokens_grad = relative(grad_mid + stream_part, f, nf)

    late_hidden = after(hidden, mid_low)
    mlp_out = scatter_sum(times_transpose(late_hidden, w_proj).reshape(nm, rows, width), NEAR)
    output = relative(stream_mid + bias_proj + mlp_out, f, nf).astype(BF16)

    mlp_pieces = jnp.stack(
        [lax.dynamic_slice_in_dim(mlp_sum, (h ^ k) * piece, piece, axis=2) for k in range(nh)]
    )
    mlp_part = scatter_sum(mlp_pieces, ("h",)).astype(BF16)
    fc_grad, proj_grad = place_mlp(me, gather(mlp_part, GROUP))

    def shards(x):
        return fsdp_order(x.astype(BF16).reshape(nf, shard, x.shape[1]))

    out_rel = relative(fsdp_sum(shards(contract_rows(attended, mid_natural))), j, nc)
    out_part = scatter_sum(jnp.stack([out_rel[:, r * hw : (r + 1) * hw] for r in range(nc)]), GROUP)
    qkv_part = fsdp_sum(shards(contract_rows(act_one_all, mixed_low)))
    mixed_part = jnp.concatenate([qkv_part, out_part], axis=1).astype(BF16)
    qkv_grad, out_grad = place_attention(me, gather(mixed_part, GROUP), hw)

    def spot(x, index, n):
        return jnp.concatenate([jnp.where(index == i, x, 0.0) for i in range(n)], axis=1)

    fc_spot = relative(spot(fc_bias_grad, m, nm), f, nf)
    qv_spot = relative(spot(qv_sums, j, nc), f, nf)
    proj_bias_grad = jnp.sum(grad, axis=0, keepdims=True)
    out_bias_grad = jnp.sum(grad_mid, axis=0, keepdims=True)
    fcs = fc_spot.shape[1] // nf

    def sum_vectors(wide, tall=None):
        chunks = [wide[:, r * shard : (r + 1) * shard] for r in range(nf)]
        if tall is not None:
            chunks = [
                jnp.concatenate([chunk, tall[:, r * fcs : (r + 1) * fcs].reshape(fb, shard)], axis=0)
                for r, chunk in enumerate(chunks)
            ]
        total = jnp.stack(chunks)
        for axis, bit in reversed(bits(("f",))):
            size = total.shape[0] // 2
            total = total[:size] + swap(total[size:], axis, bit)
        total = total[0]
        for axis, bit in bits(GROUP):
            total = total + swap(total, axis, bit)
        return total

    total = sum_vectors(
        jnp.concatenate([gain_two_grad, shift_two_grad, out_bias_grad, proj_bias_grad, qv_spot], axis=0), fc_spot
    )
    first = sum_vectors(jnp.concatenate([gain_one_grad, shift_one_grad], axis=0))

    row = lambda i: total[i : i + 1]
    return (
        output,
        tokens_grad,
        first[0:1],
        first[1:2],
        qkv_grad[None],
        total[4:6][None],
        out_grad[None],
        row(2),
        row(0),
        row(1),
        fc_grad[None],
        total[6:].reshape(1, fb * shard),
        proj_grad[None],
        row(3),
    )


def solution(mesh):
    nf, nc = mesh.shape["fsdp"], mesh.shape["ctx"]
    fine = Mesh(mesh.devices.reshape(nf, nc // 4, 2, 2), ("f", "h", "l", "c"))
    everywhere = ("f", "h", "l", "c")
    return jax.shard_map(
        body,
        mesh=fine,
        in_specs=(
            P(everywhere, None),
            P(),
            P(None, "f"),
            P(None, "f"),
            P(None, "f", None),
            P(None, None, "f"),
            P(None, "f", None),
            P(None, "f"),
            P(None, "f"),
            P(None, "f"),
            P(None, "f", None),
            P(None, "f"),
            P(None, None, "f"),
            P(None, "f"),
            P(everywhere, None),
        ),
        out_specs=(
            P(everywhere, None),
            P(everywhere, None),
            P(None, "f"),
            P(None, "f"),
            P(None, "f", None),
            P(None, None, "f"),
            P(None, "f", None),
            P(None, "f"),
            P(None, "f"),
            P(None, "f"),
            P(None, "f", None),
            P(None, "f"),
            P(None, None, "f"),
            P(None, "f"),
        ),
        check_vma=False,
    )
```
